128 devices in a mesh: rep: 4 (over y), exp: 32 (over x, z, core).
Axes of the slice: x: 4, y: 4, z: 4, core: 2. Of those that a mesh axis runs over, the one named last changes fastest.
Arguments:
- tokens: bfloat16 [16384, 3584], P(('rep', 'exp')), parts along dimension 0, may hold values from -6 to 6
- expert_ids: int32 [16384, 4], P(('rep', 'exp')), parts along dimension 0, may hold values from 0 to 31, all different within a row; in each aligned block of 128 rows (0 to 127, 128 to 255, ...) at most 24 rows name the same one
- gate_probs: float32 [16384, 4], P(('rep', 'exp')), parts along dimension 0, may hold values from 0.1 to 1
- placed: int32 [32], replicated, may hold values from 0 to 31, each once
- w_gate: bfloat16 [32, 3584, 1024], P('exp'), may hold values from -0.09375 to 0.09375
- w_up: bfloat16 [32, 3584, 1024], P('exp'), may hold values from -0.09375 to 0.09375
- w_down: bfloat16 [32, 1024, 3584], P('exp'), may hold values from -0.1875 to 0.1875
Outputs:
- mixed: bfloat16 [16384, 3584], P(('rep', 'exp')), parts along dimension 0
The draws below stay inside these ranges and needn't reach their ends.
There are 4 independent parts, one for each index of `rep`. The reference program is written for one: setup_inputs(seed, part) draws one part's arguments, and reference() takes and returns one part's arrays. A program takes and returns all parts, laid end to end along the dimension named above; an argument that names none is the same for every part. Nothing has to cross between parts.
Inputs may be any that keep to these rules, and one draw needn't show every extreme that they name: `expert_ids`: each row names 4 different experts. In the rows of one device no expert is named more than 24 times, a bound that some block reaches. `placed`: each expert once.
All inputs are finite; a program needn't handle non-finite values.
Results may differ from the reference program's by a relative error of at most 0.008.
Values may be sent and summed in bfloat16 or wider, within the bound.
A program may use at most 192 MiB of HBM per device.

```python
import math
import jax
import jax.numpy as jnp
import numpy as np
from jax import lax

D = 3584
HID = 1024
TOPK = 4
TOK_DEV = 128
EXPERTS = 32
TOKENS = 4096
CAP = 24
N_EXP = 32


def steps_of(key, extent, split, smallest, top_value):
    level, own = 1.0, jax.random.fold_in(key, 6)
    for dim, parts in split:
        draws = jnp.exp(jax.random.uniform(jax.random.fold_in(own, dim), (parts,), jnp.float32, smallest / len(split), top_value / len(split)))
        level = level * jnp.repeat(draws, extent[dim] // parts).reshape([-1 if axis == dim else 1 for axis in range(len(extent))])
    return level


def assign_block(own_key, own, number, rows, count, top, most, lean):
    order = jax.random.permutation(own_key, count)
    crowded, common = load_shares(count, rows * top, most, lean, True), load_shares(count, rows * top, most, lean, False)
    places = jnp.arange(count)

    def named(tallies, offset_by):
        used = int((tallies > 0).sum())
        fixed = max(1, used // 4)
        passed = fixed + (places - fixed + offset_by * (used - fixed)) % max(1, count - fixed)
        return jnp.zeros((count,), jnp.int32).at[order[jnp.where(places < fixed, places, passed)]].set(jnp.asarray(tallies, jnp.int32))

    tallies = jnp.where(number % 4 == 0, named(crowded, number // 4), named(common, number - number // 4 - 1))
    mixed = jax.random.permutation(jax.random.fold_in(own, 3), count)
    giver, receiver = mixed[0:count // 2 * 2:2], mixed[1:count // 2 * 2:2]
    slack = jnp.minimum(tallies[giver] - 1, most - tallies[receiver]) // 2
    slack = jnp.where((giver == order[0]) | (receiver == order[0]) | (tallies[receiver] == 0), 0, jnp.maximum(slack, 0))
    passed = jax.random.randint(jax.random.fold_in(own, 4), (count // 2,), 0, 1 << 20) % (slack + 1)
    tallies = tallies.at[giver].add(-passed).at[receiver].add(passed)
    members = jnp.searchsorted(jnp.cumsum(tallies), jnp.arange(rows * top), side="right").astype(jnp.int32)
    listing = members.reshape(top, rows).T
    listing = listing[jax.random.permutation(jax.random.fold_in(own, 1), rows)]
    offset_by = jax.random.randint(jax.random.fold_in(own, 2), (rows, 1), 0, top)
    return jnp.take_along_axis(listing, (jnp.arange(top)[None, :] + offset_by) % top, axis=1)


def load_shares(count, total, reach, slope, full):
    loads = [(1 << 20) // math.isqrt(rank ** slope) + 1 for rank in range(1, count + 1)]
    largest = reach if full else min(reach, max(-(-total // count), total * loads[0] // sum(loads)))
    least = 1 if total - largest >= count - 1 else 0
    given, surplus = [largest] + [least] * (count - 1), total - largest - least * (count - 1)
    while surplus > 0:
        movable = [i for i in range(1, count) if given[i] < largest] or [i for i in range(1, count) if given[i] < reach]
        pool, remaining = sum([loads[i] for i in movable]), surplus
        for i in movable:
            extra = min(reach - given[i], max(1, remaining * loads[i] // pool), surplus)
            given[i] = given[i] + extra
            surplus = surplus - extra
    return np.array(given)


def normal_values(own_key, extent, deviation, limit, cuts=(), kind=jnp.bfloat16):
    values = deviation * jax.random.normal(own_key, extent, jnp.float32)
    if cuts:
        values = values * steps_of(own_key, extent, cuts, -0.22, 0.18)
    return jnp.clip(values, -limit, limit).astype(kind)


def setup_inputs(seed: int = 0, part: int = 0) -> dict:
    keys = jax.random.split(jax.random.key(seed), 8)
    part_splits = jax.random.split(jax.random.fold_in(keys[7], part), 8)
    tokens = normal_values(part_splits[0], (TOKENS, D), 1.0, 6.0, ((0, 32),))
    expert_ids_keys = jax.random.split(jax.random.fold_in(part_splits[1], 1), TOKENS // TOK_DEV)
    expert_ids_turns = jax.random.permutation(jax.random.fold_in(part_splits[1], 3), TOKENS // TOK_DEV)
    expert_ids = jax.vmap(lambda own, number: assign_block(jax.random.fold_in(part_splits[1], 2), own, number, TOK_DEV, EXPERTS, TOPK, CAP, 2))(expert_ids_keys, expert_ids_turns).reshape((TOKENS, TOPK))
    gate_probs = jnp.clip(0.1 + 0.9 * jax.random.uniform(part_splits[2], (TOKENS, TOPK), jnp.float32) ** steps_of(part_splits[2], (TOKENS, TOPK), ((0, 32),), -0.2, 0.2), 0.1, 1.0)
    placed = jax.random.permutation(keys[3], EXPERTS).astype(jnp.int32)
    w_gate = normal_values(keys[4], (EXPERTS, D, HID), D ** -0.5, 0.09375, ((0, 32),))
    w_up = normal_values(keys[5], (EXPERTS, D, HID), D ** -0.5, 0.09375, ((0, 32),))
    w_down = normal_values(keys[6], (EXPERTS, HID, D), HID ** -0.5, 0.1875, ((0, 32),))
    return dict(tokens=tokens, expert_ids=expert_ids, gate_probs=gate_probs, placed=placed, w_gate=w_gate, w_up=w_up, w_down=w_down)


def reference(tokens, expert_ids, gate_probs, placed, w_gate, w_up, w_down):
    flat_ids = expert_ids.reshape(-1)
    flat_probs = gate_probs.reshape(-1)
    owner = (jnp.arange(TOKENS * TOPK, dtype=jnp.int32) // TOPK).astype(jnp.int32)
    room = N_EXP * CAP

    def one_expert(total, inputs):
        expert, gate_w, up_w, down_w = inputs
        match = flat_ids == expert
        rank = jnp.cumsum(match.astype(jnp.int32)) - 1
        where_to = jnp.where(match, rank, room).astype(jnp.int32)
        slot_tok = jnp.full((room,), TOKENS, jnp.int32).at[where_to].set(owner, mode="drop")
        slot_prob = jnp.zeros((room,), jnp.float32).at[where_to].set(flat_probs, mode="drop")
        rows = jnp.take(tokens, slot_tok, axis=0, mode="fill", fill_value=0)
        gate = jnp.dot(rows, gate_w, preferred_element_type=jnp.float32)
        up = jnp.dot(rows, up_w, preferred_element_type=jnp.float32)
        hidden = (jax.nn.silu(gate) * up).astype(jnp.bfloat16)
        result = jnp.dot(hidden, down_w, preferred_element_type=jnp.float32).astype(jnp.bfloat16)
        weighted = slot_prob[:, None] * result.astype(jnp.float32)
        total = total.at[slot_tok].add(weighted, mode="drop")
        return total, None

    start = jnp.zeros((TOKENS, D), jnp.float32)
    total, _ = lax.scan(one_expert, start, (placed, w_gate, w_up, w_down))
    return total.astype(jnp.bfloat16)
```

```python
import jax
import jax.numpy as jnp
from jax import lax
from jax.sharding import PartitionSpec as P

ROOM = 24


def body(tokens, expert_ids, gate_probs, placed, w_gate, w_up, w_down):
    rows, width = tokens.shape
    devices = lax.axis_size("exp")
    hit = placed[:, None, None] == expert_ids[None, :, :]
    named = jnp.any(hit, axis=2)
    weight = jnp.sum(jnp.where(hit, gate_probs[None, :, :], 0.0), axis=2)
    t = jnp.arange(rows, dtype=jnp.int32)
    before = (t[:, None] < t[None, :]).astype(jnp.bfloat16)
    rank = jnp.dot(named.astype(jnp.bfloat16), before, preferred_element_type=jnp.float32)
    rank = jnp.where(named, rank, -1.0).astype(jnp.int32)
    slot = jnp.arange(ROOM, dtype=jnp.int32)
    chosen = rank[:, None, :] == slot[None, :, None]
    pick = chosen.astype(jnp.bfloat16).reshape(devices * ROOM, rows)
    outgoing = jnp.dot(pick, tokens, preferred_element_type=jnp.float32).astype(jnp.bfloat16)
    received = lax.all_to_all(outgoing.reshape(devices, ROOM, width), "exp", 0, 0, tiled=True)
    flat = received.reshape(devices * ROOM, width)
    gate = jnp.dot(flat, w_gate[0], preferred_element_type=jnp.float32)
    up = jnp.dot(flat, w_up[0], preferred_element_type=jnp.float32)
    hidden = (jax.nn.silu(gate) * up).astype(jnp.bfloat16)
    produced = jnp.dot(hidden, w_down[0], preferred_element_type=jnp.float32).astype(jnp.bfloat16)
    returned = lax.all_to_all(produced.reshape(devices, ROOM, width), "exp", 0, 0, tiled=True)
    high = weight.astype(jnp.bfloat16)
    low = (weight - high.astype(jnp.float32)).astype(jnp.bfloat16)
    zero = jnp.zeros((), jnp.bfloat16)
    mix_h = jnp.where(chosen, high[:, None, :], zero).reshape(devices * ROOM, rows)
    mix_l = jnp.where(chosen, low[:, None, :], zero).reshape(devices * ROOM, rows)
    back = returned.reshape(devices * ROOM, width)
    dims = (((0,), (0,)), ((), ()))
    mixed = lax.dot_general(mix_h, back, dims, preferred_element_type=jnp.float32)
    mixed = mixed + lax.dot_general(mix_l, back, dims, preferred_element_type=jnp.float32)
    return mixed.astype(jnp.bfloat16)


def solution(mesh):
    return jax.shard_map(
        body,
        mesh=mesh,
        in_specs=(
            P(("rep", "exp"), None),
            P(("rep", "exp"), None),
            P(("rep", "exp"), None),
            P(),
            P("exp", None, None),
            P("exp", None, None),
            P("exp", None, None),
        ),
        out_specs=P(("rep", "exp"), None),
        check_vma=False,
    )
```
